32 devices in a mesh: grp: 4 (over y, x), blk: 8 (over z, core).
Axes of the slice: x: 2, y: 2, z: 4, core: 2. Of those that a mesh axis runs over, the one named last changes fastest.
Arguments:
- activations: bfloat16 [32768, 3072], P(('grp', 'blk')), may hold values from -6 to 6
- out_grads: bfloat16 [32768, 3072], P(('grp', 'blk')), may hold values from -6 to 6
- proj_act: bfloat16 [3072, 128], replicated, may hold values from -1 to 1
- proj_out: bfloat16 [3072, 256], replicated, may hold values from -0.109375 to 0.109375
Outputs:
- scores: float32 [512, 128], P(('grp', 'blk'))
The draws below stay inside these ranges and needn't reach their ends.
All inputs are finite; a program needn't handle non-finite values.
Results may differ from the reference program's by a relative error of at most 0.0012.
Values may be sent and summed in bfloat16 or wider, within the bound.
A program may use at most 128 MiB of HBM per device.

```python
import math
import jax
import jax.numpy as jnp
from jax import lax

D = 3072
RA = 128
RB = 256
SEQ = 64
ITERS = 4
EX_DEV = 16
GROUPS = 4
BLOCKS = 8
GROUP_EX = 128
EXAMPLES = 512
TOKENS = 32768
COORDS = 32768
COORD_BLK = 4096


def draw_proj_act(key, part):
    base = jnp.clip(jax.random.normal(jax.random.fold_in(key, 11), (D, RA), jnp.float32), -6.0, 6.0)
    ladder = jnp.arange(RA).astype(jnp.float32) / RA
    jitter = jax.random.uniform(jax.random.fold_in(key, 12), (RA,), jnp.float32, -0.4, 0.4)
    column = jnp.exp(ladder * math.log(3.0) + jitter)
    values = jnp.clip(base * column / math.sqrt(D), -1.0, 1.0)
    return values.astype(jnp.bfloat16)


def level_of(key, shape, pieces, smallest, top_value):
    def one(axis_at, blocks):
        steps = jax.random.uniform(jax.random.fold_in(jax.random.fold_in(key, 6), axis_at), (blocks,), jnp.float32, smallest / len(pieces), top_value / len(pieces))
        return jnp.repeat(jnp.exp(steps), shape[axis_at] // blocks).reshape((-1,) + (1,) * (len(shape) - axis_at - 1))

    loudness = one(*pieces[0])
    for cut in pieces[1:]:
        loudness = loudness * one(*cut)
    return loudness


def normal_values(own_key, shape, deviation, limit, cuts=(), held_as=jnp.bfloat16):
    values = jax.random.normal(own_key, shape, jnp.float32) * deviation
    if len(cuts) > 0:
        values = level_of(own_key, shape, cuts, -0.22, 0.18) * values
    return jnp.clip(values, min=-limit, max=limit).astype(held_as)


def setup_inputs(seed: int = 0) -> dict:
    splits = jax.random.split(jax.random.key(seed), 5)
    return {
        "activations": normal_values(splits[0], (TOKENS, D), 1.0, 6.0, ((0, 32),)),
        "out_grads": normal_values(splits[1], (TOKENS, D), 1.0, 6.0, ((0, 32),)),
        "proj_act": draw_proj_act(jax.random.fold_in(splits[4], 71), 0),
        "proj_out": normal_values(splits[3], (D, RB), D ** -0.5, 0.109375),
    }


damping_rate = 0.5
power_steps = 3

def top_estimate(gram_sum):
    width = gram_sum.shape[0]
    vector = jnp.full((width,), 1.0 / math.sqrt(width), jnp.float32)
    top = jnp.float32(1.0)
    for step in range(power_steps):
        image = jnp.dot(gram_sum, vector, precision=lax.Precision.HIGHEST)
        top = jnp.sqrt(jnp.sum(image * image) + 1e-06)
        vector = image / top
    return top

def chebyshev(gram_sum, damping, right_side):
    radius = top_estimate(gram_sum)
    center = damping + radius

    def operate(field):
        return jnp.dot(gram_sum, field, precision=lax.Precision.HIGHEST) + damping * field
    stride = 1.0 / center
    direction = right_side
    solution = stride * direction
    residual = right_side - stride * operate(direction)
    for sweep in range(1, ITERS):
        if sweep == 1:
            momentum = 0.5 * (radius * stride) ** 2
        else:
            momentum = (0.5 * radius * stride) ** 2
        stride = 1.0 / (center - momentum / stride)
        direction = residual + momentum * direction
        solution = solution + stride * direction
        if sweep + 1 < ITERS:
            residual = residual - stride * operate(direction)
    return solution

def reference(activations, out_grads, proj_act, proj_out):
    act_low = jnp.dot(activations, proj_act, preferred_element_type=jnp.float32).astype(jnp.bfloat16)
    grad_low = jnp.dot(out_grads, proj_out, preferred_element_type=jnp.float32).astype(jnp.bfloat16)
    features = jnp.einsum('etr,ets->ers', act_low.reshape(EXAMPLES, SEQ, RA).astype(jnp.float32), grad_low.reshape(EXAMPLES, SEQ, RB).astype(jnp.float32), precision=lax.Precision.HIGHEST)
    features = features.astype(jnp.bfloat16).reshape(EXAMPLES, COORDS)
    widened = features.astype(jnp.float32)
    total = jnp.sum(widened * widened)
    damping = damping_rate * total / COORDS
    grouped = features.reshape(GROUPS, GROUP_EX, BLOCKS, COORD_BLK)

    def one_block(running, block_rows):
        wide_rows = block_rows.astype(jnp.float32)
        gram_sum = jnp.einsum('gec,ged->cd', wide_rows, wide_rows, precision=lax.Precision.HIGHEST)

        def per_group(rows):
            solved = chebyshev(gram_sum, damping, rows.T)
            solved = lax.optimization_barrier(solved.astype(jnp.bfloat16)).astype(jnp.float32)
            return jnp.dot(rows, solved, precision=lax.Precision.HIGHEST)
        return (running + jax.vmap(per_group)(wide_rows), None)
    start_sum = jnp.zeros((GROUPS, GROUP_EX, GROUP_EX), jnp.float32)
    running, _ = lax.scan(one_block, start_sum, jnp.moveaxis(grouped, 2, 0))
    return running.reshape(EXAMPLES, GROUP_EX) * float(EX_DEV * GROUPS)
```

```python
import functools
import math

import jax
import jax.numpy as jnp
from jax import lax
from jax.experimental import pallas as pl
from jax.experimental.pallas import tpu as pltpu
from jax.sharding import PartitionSpec as P

SEQ = 64
ITERS = 4
damping_rate = 0.5
power_steps = 3
MESH = pl.DeviceIdType.MESH
NT = (((1,), (1,)), ((), ()))
TN = (((0,), (0,)), ((), ()))


def feature_kernel(examples, act_ref, grad_ref, feat_ref, stat_ref, wide):
    rank = act_ref.shape[1]
    for e in range(examples):
        tokens = pl.ds(e * SEQ, SEQ)
        product = lax.dot_general(
            act_ref[tokens, :], grad_ref[tokens, :], TN, preferred_element_type=jnp.float32
        )
        for c in range(wide.shape[0]):
            wide[c, pl.ds(e, rank, stride=examples), :] = product[:, c * 128:(c + 1) * 128]

    def step(i, acc):
        rows = pl.ds(pl.multiple_of(i * 128, 128), 128)
        for c in range(wide.shape[0]):
            low = wide[c, rows, :].astype(jnp.bfloat16)
            feat_ref[rows, c * 128:(c + 1) * 128] = low
            back = low.astype(jnp.float32)
            acc += back * back
        return acc

    acc = lax.fori_loop(0, wide.shape[1] // 128, step, jnp.zeros((128, 128), jnp.float32))
    stat_ref[...] = jnp.broadcast_to(jnp.sum(acc, keepdims=True), stat_ref.shape)


def mix_kernel(
    groups, blocks, examples, ranks, width,
    feat_ref, stat_ref, out_ref,
    recv, stats, part, landed, full, prow_part, prow_land, row, col, col_next,
    y_ref, sc, sc_land,
    f_send, f_recv, t_send, t_recv, r_send, r_recv, g_send, g_recv, p_send, p_recv, s_send, s_recv,
):
    devices = groups * blocks
    group_ex = examples * blocks
    total_ex = group_ex * groups
    span = recv.shape[2]
    rows_out = ranks * examples
    grp, blk = lax.axis_index("grp"), lax.axis_index("blk")
    me = grp * blocks + blk

    def peer_of(d):
        peer = lax.rem(me + d, devices)
        return peer, peer // blocks, lax.rem(peer, blocks)

    barrier = pltpu.get_barrier_semaphore()

    def greet(d, c):
        _, pg, pb = peer_of(d)
        pl.semaphore_signal(barrier, inc=1, device_id=(pg, pb), device_id_type=MESH)
        return c

    lax.fori_loop(1, devices, greet, 0)
    pl.semaphore_wait(barrier, devices - 1)

    def feature_copy(dest, pg, pb, slot):
        start = pl.multiple_of((pb * groups + pg) * rows_out, rows_out)
        return pltpu.make_async_remote_copy(
            src_ref=feat_ref.at[pl.ds(start, rows_out)], dst_ref=recv.at[slot],
            send_sem=f_send.at[dest], recv_sem=f_recv.at[slot],
            device_id=(pg, pb), device_id_type=MESH)

    def stat_copy(dest, pg, pb, slot):
        return pltpu.make_async_remote_copy(
            src_ref=stat_ref, dst_ref=stats.at[slot],
            send_sem=t_send.at[dest], recv_sem=t_recv.at[slot],
            device_id=(pg, pb), device_id_type=MESH)

    def send(d, c):
        peer, pg, pb = peer_of(d)
        feature_copy(peer, pg, pb, me).start()
        return c

    lax.fori_loop(1, devices, send, 0)

    def send_stat(d, c):
        peer, pg, pb = peer_of(d)
        stat_copy(peer, pg, pb, me).start()
        return c

    lax.fori_loop(1, devices, send_stat, 0)
    own = pl.multiple_of((blk * groups + grp) * rows_out, rows_out)
    recv[me] = feat_ref[pl.ds(own, rows_out), :]
    stats[me] = stat_ref[...]

    def arrive(d, c):
        peer, pg, pb = peer_of(d)
        feature_copy(peer, pg, pb, peer).wait_recv()
        return c

    lax.fori_loop(1, devices, arrive, 0)

    def grp_rows(h):
        return pl.ds(pl.multiple_of(h * group_ex, group_ex), group_ex)

    def part_rows(h):
        for r in range(ranks):
            here = pl.ds(r * examples, examples)
            left = recv[pl.ds(h * blocks, blocks), here, :].reshape(group_ex, span)
            for c in range(groups):
                right = recv[c * blocks:(c + 1) * blocks, here, :].reshape(group_ex, span)
                term = lax.dot_general(left, right, NT, preferred_element_type=jnp.float32)
                cols = slice(c * group_ex, (c + 1) * group_ex)
                if r == 0:
                    part[grp_rows(h), cols] = term
                else:
                    part[grp_rows(h), cols] += term

    def part_copy(h, slot):
        return pltpu.make_async_remote_copy(
            src_ref=part.at[grp_rows(h)], dst_ref=landed.at[slot],
            send_sem=r_send.at[h], recv_sem=r_recv.at[slot],
            device_id=(h, blk), device_id_type=MESH)

    def full_copy(h, slot):
        return pltpu.make_async_remote_copy(
            src_ref=full.at[grp_rows(slot)], dst_ref=full.at[grp_rows(slot)],
            send_sem=g_send.at[h], recv_sem=g_recv.at[slot],
            device_id=(h, blk), device_id_type=MESH)

    def prow_copy(h, slot):
        return pltpu.make_async_remote_copy(
            src_ref=prow_part, dst_ref=prow_land.at[slot],
            send_sem=p_send.at[h], recv_sem=p_recv.at[slot],
            device_id=(h, blk), device_id_type=MESH)

    others = [lax.rem(grp + d, groups) for d in range(1, groups)]

    def part_step(d, c):
        h = lax.rem(grp + d, groups)
        part_rows(h)
        part_copy(h, grp).start()
        return c

    lax.fori_loop(1, groups, part_step, 0)
    part_rows(grp)

    ones = jnp.ones((8, span), jnp.bfloat16)
    scale = 1.0 / math.sqrt(width)
    for c in range(groups):
        cols = slice(c * group_ex, (c + 1) * group_ex)
        acc = jnp.zeros((8, group_ex), jnp.float32)
        for r in range(ranks):
            right = recv[c * blocks:(c + 1) * blocks, pl.ds(r * examples, examples), :]
            acc += lax.dot_general(
                ones, right.reshape(group_ex, span), NT, preferred_element_type=jnp.float32)
        prow_part[:, cols] = acc * scale
    for h in others:
        prow_copy(h, grp).start()

    for h in others:
        part_copy(h, h).wait_recv()
    mine = part[grp_rows(grp), :]
    for h in others:
        mine += landed[h]
    full[grp_rows(grp), :] = mine
    for h in others:
        full_copy(h, grp).start()

    def arrive_stat(d, c):
        peer, pg, pb = peer_of(d)
        stat_copy(peer, pg, pb, peer).wait_recv()
        return c

    lax.fori_loop(1, devices, arrive_stat, 0)
    total = jnp.sum(stats[...], axis=0)[:1, :1]
    damping = damping_rate * total / (width * blocks)
    for h in others:
        prow_copy(h, h).wait_recv()
    first = prow_part[...]
    for h in others:
        first += prow_land[h]
    row[...] = first
    for h in others:
        full_copy(h, h).wait_recv()

    tile = 128
    tiles = total_ex // tile

    def tile_rows(i):
        return pl.ds(pl.multiple_of(i * tile, tile), tile)

    def turn(i, c):
        spot = lax.broadcasted_iota(jnp.int32, (tile, total_ex), 0) + i * tile
        lane = lax.broadcasted_iota(jnp.int32, (tile, total_ex), 1)
        picked = jnp.where(spot == lane, row[:1, :], 0.0)
        col[tile_rows(i), :] = jnp.broadcast_to(
            jnp.sum(picked, axis=1, keepdims=True), (tile, 128))
        return c

    lax.fori_loop(0, tiles, turn, 0)
    top = None
    for step in range(power_steps):
        last = step + 1 == power_steps
        prow = row[:1, :]

        def image(i, acc):
            k_tile = full[tile_rows(i), :]
            if not last:
                col_next[tile_rows(i), :] = jnp.broadcast_to(
                    jnp.sum(k_tile * prow, axis=1, keepdims=True), (tile, 128))
            return acc + jnp.sum(k_tile * col[tile_rows(i), :][:, :1], axis=0, keepdims=True)

        q = lax.fori_loop(0, tiles, image, jnp.zeros((1, total_ex), jnp.float32))
        square = jnp.sum(prow * q, axis=1, keepdims=True)
        top = jnp.sqrt(jnp.maximum(square, 0.0) + 1e-06)
        if not last:
            row[...] = jnp.broadcast_to(q / top, row.shape)
            col[...] = col_next[...] / top

    center = damping + top
    rho, delta = top / center, damping / center
    zero, one = jnp.zeros_like(center), jnp.ones_like(center)

    def shifted(p):
        low = [delta * v for v in p] + [zero]
        return [a + b for a, b in zip(low, [zero] + list(p))]

    def plus(p, q, factor):
        n = max(len(p), len(q))
        p = list(p) + [zero] * (n - len(p))
        q = list(q) + [zero] * (n - len(q))
        return [a + factor * b for a, b in zip(p, q)]

    sig = one
    direction = [one]
    solution_poly = [one]
    residual = plus([one], shifted(direction), -sig)
    for sweep in range(1, ITERS):
        momentum = 0.5 * (rho * sig) ** 2 if sweep == 1 else (0.5 * rho * sig) ** 2
        sig = 1.0 / (1.0 - momentum / sig)
        direction = plus(residual, direction, momentum)
        solution_poly = plus(solution_poly, direction, sig)
        if sweep + 1 < ITERS:
            residual = plus(residual, shifted(direction), -sig)
    s0, s1, s2, s3 = solution_poly

    inverse = 1.0 / center
    y_ref[...] = full[grp_rows(grp), :] * inverse
    own_cols = pl.ds(pl.multiple_of(grp * group_ex, group_ex), group_ex)
    sc[...] = s0 * y_ref[:, own_cols]
    wide = min(256, total_ex)

    def dot_nt(a, b):
        return lax.dot_general(a, b, NT, precision=lax.Precision.HIGHEST,
                               preferred_element_type=jnp.float32)

    def solve(j, c):
        at = pl.ds(pl.multiple_of(j * wide, wide), wide)
        y_tile = y_ref[:, at]
        z_tile = dot_nt(y_ref[...], full[at, :] * inverse)
        sc[...] += dot_nt(y_tile, s1 * y_tile + s2 * z_tile) + dot_nt(z_tile, s3 * z_tile)
        return c

    lax.fori_loop(0, total_ex // wide, solve, 0)

    def score_copy(b, slot):
        start = pl.multiple_of(b * examples, examples)
        return pltpu.make_async_remote_copy(
            src_ref=sc.at[pl.ds(start, examples)], dst_ref=sc_land.at[slot],
            send_sem=s_send.at[b], recv_sem=s_recv.at[slot],
            device_id=(grp, b), device_id_type=MESH)

    def score_send(d, c):
        b = lax.rem(blk + d, blocks)
        score_copy(b, blk).start()
        return c

    lax.fori_loop(1, blocks, score_send, 0)
    sc_land[blk] = sc[pl.ds(pl.multiple_of(blk * examples, examples), examples), :]

    def score_arrive(d, c):
        b = lax.rem(blk + d, blocks)
        score_copy(b, b).wait_recv()
        return c

    lax.fori_loop(1, blocks, score_arrive, 0)
    out_ref[...] = jnp.sum(sc_land[...], axis=0) * float(examples * groups)

    def sent(d, c):
        peer, pg, pb = peer_of(d)
        feature_copy(peer, pg, pb, me).wait_send()
        stat_copy(peer, pg, pb, me).wait_send()
        return c

    lax.fori_loop(1, devices, sent, 0)
    for h in others:
        part_copy(h, grp).wait_send()
        full_copy(h, grp).wait_send()
        prow_copy(h, grp).wait_send()

    def score_sent(d, c):
        score_copy(lax.rem(blk + d, blocks), blk).wait_send()
        return c

    lax.fori_loop(1, blocks, score_sent, 0)


def shards(groups, blocks, activations, out_grads, proj_act, proj_out):
    examples = activations.shape[0] // SEQ
    rank, span = proj_act.shape[1], proj_out.shape[1]
    devices = groups * blocks
    group_ex, total_ex = examples * blocks, examples * devices
    ranks = rank // devices
    width = rank * span // blocks
    act_low = jnp.dot(activations, proj_act, preferred_element_type=jnp.float32).astype(
        jnp.bfloat16
    )
    grad_low = jnp.dot(out_grads, proj_out, preferred_element_type=jnp.float32).astype(jnp.bfloat16)
    vmem = pl.BlockSpec(memory_space=pltpu.VMEM)
    features, stat = pl.pallas_call(
        functools.partial(feature_kernel, examples),
        out_shape=(
            jax.ShapeDtypeStruct((rank * examples, span), jnp.bfloat16),
            jax.ShapeDtypeStruct((8, 128), jnp.float32),
        ),
        in_specs=[vmem] * 2,
        out_specs=(vmem, vmem),
        scratch_shapes=[pltpu.VMEM((span // 128, rank * examples, 128), jnp.float32)],
    )(act_low, grad_low)

    f32 = jnp.float32
    dma = pltpu.SemaphoreType.DMA
    return pl.pallas_call(
        functools.partial(mix_kernel, groups, blocks, examples, ranks, width),
        out_shape=jax.ShapeDtypeStruct((examples, group_ex), f32),
        in_specs=[vmem] * 2,
        out_specs=vmem,
        scratch_shapes=[
            pltpu.VMEM((devices, ranks * examples, span), jnp.bfloat16),
            pltpu.VMEM((devices, 8, 128), f32),
            pltpu.VMEM((total_ex, total_ex), f32),
            pltpu.VMEM((groups, group_ex, total_ex), f32),
            pltpu.VMEM((total_ex, total_ex), f32),
            pltpu.VMEM((8, total_ex), f32),
            pltpu.VMEM((groups, 8, total_ex), f32),
            pltpu.VMEM((8, total_ex), f32),
            pltpu.VMEM((total_ex, 128), f32),
            pltpu.VMEM((total_ex, 128), f32),
            pltpu.VMEM((group_ex, total_ex), f32),
            pltpu.VMEM((group_ex, group_ex), f32),
            pltpu.VMEM((blocks, examples, group_ex), f32),
            dma((devices,)), dma((devices,)), dma((devices,)), dma((devices,)),
            dma((groups,)), dma((groups,)), dma((groups,)), dma((groups,)),
            dma((groups,)), dma((groups,)), dma((blocks,)), dma((blocks,)),
        ],
        compiler_params=pltpu.CompilerParams(
            collective_id=0, has_side_effects=True, vmem_limit_bytes=67043328
        ),
    )(features, stat)


def solution(mesh):
    in_specs = (P(("grp", "blk"), None), P(("grp", "blk"), None), P(), P())
    out_specs = P(("grp", "blk"), None)
    body = functools.partial(shards, mesh.shape["grp"], mesh.shape["blk"])
    return jax.shard_map(body, mesh=mesh, in_specs=in_specs, out_specs=out_specs, check_vma=False)
```

```python
import functools
import math

import jax
import jax.numpy as jnp
from jax import lax
from jax.experimental import pallas as pl
from jax.experimental.pallas import tpu as pltpu
from jax.sharding import PartitionSpec as P

SEQ = 64
ITERS = 4
damping_rate = 0.5
power_steps = 3
MESH = pl.DeviceIdType.MESH
NT = (((1,), (1,)), ((), ()))
TN = (((0,), (0,)), ((), ()))


def mix_kernel(
    groups, blocks, examples, ranks, width,
    act_ref, grad_ref, out_ref,
    wide, feat_ref, stat_ref, recv, stats, part, landed, packs, full, prow_part, prow_land, row, col, col_next,
    y_ref, sc, sc_land,
    f_send, f_recv, t_send, t_recv, r_send, r_recv, g_send, g_recv, p_send, p_recv, s_send, s_recv,
):
    devices = groups * blocks
    group_ex = examples * blocks
    total_ex = group_ex * groups
    span = recv.shape[2]
    rows_out = ranks * examples
    grp, blk = lax.axis_index("grp"), lax.axis_index("blk")
    me = grp * blocks + blk

    half = blocks // 2 * groups

    def peer_of(d):
        pg = lax.rem(grp + lax.rem(d, groups), groups)
        pb = lax.rem(blk + blocks // 2 + d // groups, blocks)
        return pg * blocks + pb, pg, pb

    def over_peers(step):
        lax.fori_loop(0, half, step, 0)
        lax.fori_loop(half + 1, devices, step, 0)

    barrier = pltpu.get_barrier_semaphore()

    def greet(d, c):
        _, pg, pb = peer_of(d)
        pl.semaphore_signal(barrier, inc=1, device_id=(pg, pb), device_id_type=MESH)
        return c

    over_peers(greet)
    for e in range(examples):
        tokens = pl.ds(e * SEQ, SEQ)
        product = lax.dot_general(
            act_ref[tokens, :], grad_ref[tokens, :], TN, preferred_element_type=jnp.float32
        )
        for c in range(wide.shape[0]):
            wide[c, pl.ds(e, act_ref.shape[1], stride=examples), :] = (
                product[:, c * 128:(c + 1) * 128])
    stat_ref[...] = jnp.zeros_like(stat_ref)
    pl.semaphore_wait(barrier, devices - 1)

    def feature_copy(dest, pg, pb, slot):
        return pltpu.make_async_remote_copy(
            src_ref=feat_ref.at[pb * groups + pg], dst_ref=recv.at[slot],
            send_sem=f_send.at[dest], recv_sem=f_recv.at[slot],
            device_id=(pg, pb), device_id_type=MESH)

    def stat_copy(dest, pg, pb, slot):
        return pltpu.make_async_remote_copy(
            src_ref=stat_ref, dst_ref=stats.at[slot],
            send_sem=t_send.at[dest], recv_sem=t_recv.at[slot],
            device_id=(pg, pb), device_id_type=MESH)

    def narrow(pg, pb):
        slot = pb * groups + pg
        rows = pl.ds(pl.multiple_of(slot * rows_out, rows_out), rows_out)
        for c in range(wide.shape[0]):
            low = wide[c, rows, :].astype(jnp.bfloat16)
            feat_ref[slot, :, c * 128:(c + 1) * 128] = low
            back = low.astype(jnp.float32)
            square = jnp.sum(back * back, axis=0, keepdims=True)
            stat_ref[...] += jnp.broadcast_to(square, stat_ref.shape)

    def send(d, c):
        peer, pg, pb = peer_of(d)
        narrow(pg, pb)
        feature_copy(peer, pg, pb, me).start()
        return c

    over_peers(send)
    narrow(grp, blk)
    recv[me] = feat_ref[blk * groups + grp]

    def send_stat(d, c):
        peer, pg, pb = peer_of(d)
        stat_copy(peer, pg, pb, me).start()
        return c

    over_peers(send_stat)
    stats[me] = stat_ref[...]

    def arrive(d, c):
        peer, pg, pb = peer_of(d)
        feature_copy(peer, pg, pb, peer).wait_recv()
        return c

    over_peers(arrive)

    def grp_rows(h):
        return pl.ds(pl.multiple_of(h * group_ex, group_ex), group_ex)

    split = groups % 2 == 0
    whole_blocks = (groups - 1) // 2 + 1
    pair = groups // 2
    half_ex = group_ex // 2

    def block_into(h, at, left_at, left_n, right_at):
        for r in range(ranks):
            here = pl.ds(r * examples, examples)
            left = recv[pl.ds(left_at, left_n), here, :].reshape(left_n * examples, span)
            right = recv[pl.ds(right_at, blocks), here, :].reshape(group_ex, span)
            term = lax.dot_general(left, right, NT, preferred_element_type=jnp.float32)
            if r == 0:
                part[h, at:at + left_n * examples, :] = term
            else:
                part[h, at:at + left_n * examples, :] += term

    def part_of(h):
        for d in range(whole_blocks):
            block_into(h, d * group_ex, h * blocks, blocks, lax.rem(h + d, groups) * blocks)
        if split:
            low = lax.rem(h, pair)
            block_into(h, whole_blocks * group_ex,
                       low * blocks + h // pair * (blocks // 2), blocks // 2,
                       (low + pair) * blocks)

    def part_copy(h, d, slot):
        return pltpu.make_async_remote_copy(
            src_ref=part.at[h], dst_ref=landed.at[slot],
            send_sem=r_send.at[d], recv_sem=r_recv.at[slot],
            device_id=(h, blk), device_id_type=MESH)

    def full_copy(h, slot):
        return pltpu.make_async_remote_copy(
            src_ref=packs.at[slot], dst_ref=packs.at[slot],
            send_sem=g_send.at[h], recv_sem=g_recv.at[slot],
            device_id=(h, blk), device_id_type=MESH)

    def prow_copy(h, slot):
        return pltpu.make_async_remote_copy(
            src_ref=prow_part, dst_ref=prow_land.at[slot],
            send_sem=p_send.at[h], recv_sem=p_recv.at[slot],
            device_id=(h, blk), device_id_type=MESH)

    others = [lax.rem(grp + d, groups) for d in range(1, groups)]

    def part_step(d, c):
        h = lax.rem(grp + d, groups)
        part_of(h)
        part_copy(h, d, groups - d - 1).start()
        return c

    lax.fori_loop(1, groups, part_step, 0)
    part_of(grp)

    ones = jnp.ones((8, span), jnp.bfloat16)
    scale = 1.0 / math.sqrt(width)
    for c in range(groups):
        cols = slice(c * group_ex, (c + 1) * group_ex)
        acc = jnp.zeros((8, group_ex), jnp.float32)
        for r in range(ranks):
            right = recv[c * blocks:(c + 1) * blocks, pl.ds(r * examples, examples), :]
            acc += lax.dot_general(
                ones, right.reshape(group_ex, span), NT, preferred_element_type=jnp.float32)
        prow_part[:, cols] = acc * scale
    for h in others:
        prow_copy(h, grp).start()

    for d, h in enumerate(others):
        part_copy(h, d + 1, d).wait_recv()
    mine = part[grp]
    for d in range(groups - 1):
        mine += landed[d]
    packs[grp] = mine
    for h in others:
        full_copy(h, grp).start()

    def arrive_stat(d, c):
        peer, pg, pb = peer_of(d)
        stat_copy(peer, pg, pb, peer).wait_recv()
        return c

    over_peers(arrive_stat)
    total = jnp.sum(jnp.sum(stats[...], axis=0)[:1, :], axis=1, keepdims=True)
    damping = damping_rate * total / (width * blocks)
    for h in others:
        prow_copy(h, h).wait_recv()
    first = prow_part[...]
    for h in others:
        first += prow_land[h]
    row[...] = first
    for h in others:
        full_copy(h, h).wait_recv()
    for o in range(groups):
        here = slice(o * group_ex, (o + 1) * group_ex)
        for d in range(whole_blocks):
            there = (o + d) % groups
            there = slice(there * group_ex, (there + 1) * group_ex)
            entry = packs[o, d * group_ex:(d + 1) * group_ex, :]
            full[here, there] = entry
            if d:
                full[there, here] = entry.T
        if split:
            low = o % pair
            start = low * group_ex + o // pair * half_ex
            there = slice((low + pair) * group_ex, (low + pair + 1) * group_ex)
            entry = packs[o, whole_blocks * group_ex:, :]
            full[start:start + half_ex, there] = entry
            full[there, start:start + half_ex] = entry.T

    tile = 128
    tiles = total_ex // tile

    def tile_rows(i):
        return pl.ds(pl.multiple_of(i * tile, tile), tile)

    def turn(i, c):
        spot = lax.broadcasted_iota(jnp.int32, (tile, total_ex), 0) + i * tile
        lane = lax.broadcasted_iota(jnp.int32, (tile, total_ex), 1)
        picked = jnp.where(spot == lane, row[:1, :], 0.0)
        col[tile_rows(i), :] = jnp.broadcast_to(
            jnp.sum(picked, axis=1, keepdims=True), (tile, 128))
        return c

    lax.fori_loop(0, tiles, turn, 0)
    top = None
    for step in range(power_steps):
        last = step + 1 == power_steps
        prow = row[:1, :]

        def image(i, acc):
            k_tile = full[tile_rows(i), :]
            if not last:
                col_next[tile_rows(i), :] = jnp.broadcast_to(
                    jnp.sum(k_tile * prow, axis=1, keepdims=True), (tile, 128))
            return acc + jnp.sum(k_tile * col[tile_rows(i), :][:, :1], axis=0, keepdims=True)

        q = lax.fori_loop(0, tiles, image, jnp.zeros((1, total_ex), jnp.float32))
        square = jnp.sum(prow * q, axis=1, keepdims=True)
        top = jnp.sqrt(jnp.maximum(square, 0.0) + 1e-06)
        if not last:
            row[...] = jnp.broadcast_to(q / top, row.shape)
            col[...] = col_next[...] / top

    center = damping + top
    rho, delta = top / center, damping / center
    zero, one = jnp.zeros_like(center), jnp.ones_like(center)

    def shifted(p):
        low = [delta * v for v in p] + [zero]
        return [a + b for a, b in zip(low, [zero] + list(p))]

    def plus(p, q, factor):
        n = max(len(p), len(q))
        p = list(p) + [zero] * (n - len(p))
        q = list(q) + [zero] * (n - len(q))
        return [a + factor * b for a, b in zip(p, q)]

    sig = one
    direction = [one]
    solution_poly = [one]
    residual = plus([one], shifted(direction), -sig)
    for sweep in range(1, ITERS):
        momentum = 0.5 * (rho * sig) ** 2 if sweep == 1 else (0.5 * rho * sig) ** 2
        sig = 1.0 / (1.0 - momentum / sig)
        direction = plus(residual, direction, momentum)
        solution_poly = plus(solution_poly, direction, sig)
        if sweep + 1 < ITERS:
            residual = plus(residual, shifted(direction), -sig)
    s0, s1, s2, s3 = solution_poly

    inverse = 1.0 / center
    y_ref[...] = full[grp_rows(grp), :] * inverse
    own_cols = pl.ds(pl.multiple_of(grp * group_ex, group_ex), group_ex)
    sc[...] = s0 * y_ref[:, own_cols]
    step_ex = min(256, total_ex)

    def dot_nt(a, b):
        return lax.dot_general(a, b, NT, precision=lax.Precision.HIGHEST,
                               preferred_element_type=jnp.float32)

    def solve(j, c):
        at = pl.ds(pl.multiple_of(j * step_ex, step_ex), step_ex)
        y_tile = y_ref[:, at]
        z_tile = dot_nt(y_ref[...], full[at, :] * inverse)
        sc[...] += dot_nt(y_tile, s1 * y_tile + s2 * z_tile) + dot_nt(z_tile, s3 * z_tile)
        return c

    lax.fori_loop(0, total_ex // step_ex, solve, 0)

    def score_copy(b, slot):
        start = pl.multiple_of(b * examples, examples)
        return pltpu.make_async_remote_copy(
            src_ref=sc.at[pl.ds(start, examples)], dst_ref=sc_land.at[slot],
            send_sem=s_send.at[b], recv_sem=s_recv.at[slot],
            device_id=(grp, b), device_id_type=MESH)

    def score_send(d, c):
        b = lax.rem(blk + d, blocks)
        score_copy(b, blk).start()
        return c

    lax.fori_loop(1, blocks, score_send, 0)
    sc_land[blk] = sc[pl.ds(pl.multiple_of(blk * examples, examples), examples), :]

    def score_arrive(d, c):
        b = lax.rem(blk + d, blocks)
        score_copy(b, b).wait_recv()
        return c

    lax.fori_loop(1, blocks, score_arrive, 0)
    out_ref[...] = jnp.sum(sc_land[...], axis=0)

    def sent(d, c):
        peer, pg, pb = peer_of(d)
        feature_copy(peer, pg, pb, me).wait_send()
        stat_copy(peer, pg, pb, me).wait_send()
        return c

    over_peers(sent)
    for d, h in enumerate(others):
        part_copy(h, d + 1, d).wait_send()
    for h in others:
        full_copy(h, grp).wait_send()
        prow_copy(h, grp).wait_send()

    def score_sent(d, c):
        score_copy(lax.rem(blk + d, blocks), blk).wait_send()
        return c

    lax.fori_loop(1, blocks, score_sent, 0)


def shards(groups, blocks, activations, out_grads, proj_act, proj_out):
    examples = activations.shape[0] // SEQ
    rank, span = proj_act.shape[1], proj_out.shape[1]
    devices = groups * blocks
    group_ex, total_ex = examples * blocks, examples * devices
    ranks = rank // devices
    width = rank * span // blocks
    act_low = jnp.dot(activations, proj_act, preferred_element_type=jnp.float32).astype(
        jnp.bfloat16
    )
    grad_low = jnp.dot(out_grads, proj_out, preferred_element_type=jnp.float32).astype(jnp.bfloat16)
    vmem = pl.BlockSpec(memory_space=pltpu.VMEM)
    f32 = jnp.float32
    dma = pltpu.SemaphoreType.DMA
    keep = group_ex * ((groups - 1) // 2 + 1) + (0 if groups % 2 else group_ex // 2)
    scores = pl.pallas_call(
        functools.partial(mix_kernel, groups, blocks, examples, ranks, width),
        out_shape=jax.ShapeDtypeStruct((examples, group_ex), f32),
        in_specs=[vmem] * 2,
        out_specs=vmem,
        scratch_shapes=[
            pltpu.VMEM((span // 128, rank * examples, 128), f32),
            pltpu.VMEM((devices, ranks * examples, span), jnp.bfloat16),
            pltpu.VMEM((8, 128), f32),
            pltpu.VMEM((devices, ranks * examples, span), jnp.bfloat16),
            pltpu.VMEM((devices, 8, 128), f32),
            pltpu.VMEM((groups, keep, group_ex), f32),
            pltpu.VMEM((groups - 1, keep, group_ex), f32),
            pltpu.VMEM((groups, keep, group_ex), f32),
            pltpu.VMEM((total_ex, total_ex), f32),
            pltpu.VMEM((8, total_ex), f32),
            pltpu.VMEM((groups, 8, total_ex), f32),
            pltpu.VMEM((8, total_ex), f32),
            pltpu.VMEM((total_ex, 128), f32),
            pltpu.VMEM((total_ex, 128), f32),
            pltpu.VMEM((group_ex, total_ex), f32),
            pltpu.VMEM((group_ex, group_ex), f32),
            pltpu.VMEM((blocks, examples, group_ex), f32),
            dma((devices,)), dma((devices,)), dma((devices,)), dma((devices,)),
            dma((groups,)), dma((groups,)), dma((groups,)), dma((groups,)),
            dma((groups,)), dma((groups,)), dma((blocks,)), dma((blocks,)),
        ],
        compiler_params=pltpu.CompilerParams(
            collective_id=0, has_side_effects=True, vmem_limit_bytes=67043328
        ),
    )(act_low, grad_low)
    return scores * float(examples * groups)


def solution(mesh):
    in_specs = (P(("grp", "blk"), None), P(("grp", "blk"), None), P(), P())
    out_specs = P(("grp", "blk"), None)
    body = functools.partial(shards, mesh.shape["grp"], mesh.shape["blk"])
    return jax.shard_map(body, mesh=mesh, in_specs=in_specs, out_specs=out_specs, check_vma=False)
```

```python
import functools
import math

import jax
import jax.numpy as jnp
from jax import lax
from jax.experimental import pallas as pl
from jax.experimental.pallas import tpu as pltpu
from jax.sharding import PartitionSpec as P

SEQ = 64
ITERS = 4
damping_rate = 0.5
power_steps = 3
MESH = pl.DeviceIdType.MESH
NT = (((1,), (1,)), ((), ()))
TN = (((0,), (0,)), ((), ()))


def mix_kernel(
    groups, blocks, examples, ranks, width,
    act_ref, grad_ref, out_ref,
    wide, feat_ref, stat_ref, recv, stats, part, landed, packs, full, prow_part, prow_land, row, col, col_next,
    y_ref, sc, sc_land,
    f_send, f_recv, t_send, t_recv, r_send, r_recv, g_send, g_recv, p_send, p_recv, s_send, s_recv,
):
    devices = groups * blocks
    group_ex = examples * blocks
    total_ex = group_ex * groups
    span = recv.shape[2]
    rows_out = ranks * examples
    grp, blk = lax.axis_index("grp"), lax.axis_index("blk")
    me = grp * blocks + blk

    half = blocks // 2 * groups

    def peer_of(d):
        pg = lax.rem(grp + lax.rem(d, groups), groups)
        pb = lax.rem(blk + blocks // 2 + d // groups, blocks)
        return pg * blocks + pb, pg, pb

    def over_peers(step):
        lax.fori_loop(0, half, step, 0)
        lax.fori_loop(half + 1, devices, step, 0)

    barrier = pltpu.get_barrier_semaphore()

    def greet(d, c):
        _, pg, pb = peer_of(d)
        pl.semaphore_signal(barrier, inc=1, device_id=(pg, pb), device_id_type=MESH)
        return c

    over_peers(greet)
    for e in range(examples):
        tokens = pl.ds(e * SEQ, SEQ)
        product = lax.dot_general(
            act_ref[tokens, :], grad_ref[tokens, :], TN, preferred_element_type=jnp.float32
        )
        for c in range(wide.shape[0]):
            wide[c, pl.ds(e, act_ref.shape[1], stride=examples), :] = (
                product[:, c * 128:(c + 1) * 128])
    stat_ref[...] = jnp.zeros_like(stat_ref)
    pl.semaphore_wait(barrier, devices - 1)

    def feature_copy(dest, pg, pb, slot):
        return pltpu.make_async_remote_copy(
            src_ref=feat_ref.at[pb * groups + pg], dst_ref=recv.at[slot],
            send_sem=f_send.at[dest], recv_sem=f_recv.at[slot],
            device_id=(pg, pb), device_id_type=MESH)

    def stat_copy(dest, pg, pb, slot):
        return pltpu.make_async_remote_copy(
            src_ref=stat_ref, dst_ref=stats.at[slot],
            send_sem=t_send.at[dest], recv_sem=t_recv.at[slot],
            device_id=(pg, pb), device_id_type=MESH)

    def narrow(pg, pb):
        slot = pb * groups + pg
        rows = pl.ds(pl.multiple_of(slot * rows_out, rows_out), rows_out)
        for c in range(wide.shape[0]):
            low = wide[c, rows, :].astype(jnp.bfloat16)
            feat_ref[slot, :, c * 128:(c + 1) * 128] = low
            back = low.astype(jnp.float32)
            square = jnp.sum(back * back, axis=0, keepdims=True)
            stat_ref[...] += jnp.broadcast_to(square, stat_ref.shape)

    def send(d, c):
        peer, pg, pb = peer_of(d)
        narrow(pg, pb)
        feature_copy(peer, pg, pb, me).start()
        return c

    over_peers(send)
    narrow(grp, blk)
    recv[me] = feat_ref[blk * groups + grp]

    def send_stat(d, c):
        peer, pg, pb = peer_of(d)
        stat_copy(peer, pg, pb, me).start()
        return c

    over_peers(send_stat)
    stats[me] = stat_ref[...]

    def arrive(d, c):
        peer, pg, pb = peer_of(d)
        feature_copy(peer, pg, pb, peer).wait_recv()
        return c

    over_peers(arrive)

    def grp_rows(h):
        return pl.ds(pl.multiple_of(h * group_ex, group_ex), group_ex)

    split = groups % 2 == 0
    whole_blocks = (groups - 1) // 2 + 1
    pair = groups // 2
    half_ex = group_ex // 2

    def block_into(h, at, left_at, left_n, right_at):
        for r in range(ranks):
            here = pl.ds(r * examples, examples)
            left = recv[pl.ds(left_at, left_n), here, :].reshape(left_n * examples, span)
            right = recv[pl.ds(right_at, blocks), here, :].reshape(group_ex, span)
            term = lax.dot_general(left, right, NT, preferred_element_type=jnp.float32)
            if r == 0:
                part[h, at:at + left_n * examples, :] = term
            else:
                part[h, at:at + left_n * examples, :] += term

    def part_of(h, q):
        for d in range(1) if q == 0 else range(1, whole_blocks):
            block_into(h, d * group_ex, h * blocks, blocks, lax.rem(h + d, groups) * blocks)
        if split and q == 1:
            low = lax.rem(h, pair)
            block_into(h, whole_blocks * group_ex,
                       low * blocks + h // pair * (blocks // 2), blocks // 2,
                       (low + pair) * blocks)

    cuts = (slice(0, group_ex), slice(group_ex, part.shape[1]))

    def part_copy(h, d, slot, q):
        return pltpu.make_async_remote_copy(
            src_ref=part.at[h, cuts[q]], dst_ref=landed.at[slot, cuts[q]],
            send_sem=r_send.at[2 * d + q], recv_sem=r_recv.at[2 * slot + q],
            device_id=(h, blk), device_id_type=MESH)

    def full_copy(h, slot, q):
        return pltpu.make_async_remote_copy(
            src_ref=packs.at[slot, cuts[q]], dst_ref=packs.at[slot, cuts[q]],
            send_sem=g_send.at[2 * h + q], recv_sem=g_recv.at[2 * slot + q],
            device_id=(h, blk), device_id_type=MESH)

    def prow_copy(h, slot):
        return pltpu.make_async_remote_copy(
            src_ref=prow_part, dst_ref=prow_land.at[slot],
            send_sem=p_send.at[h], recv_sem=p_recv.at[slot],
            device_id=(h, blk), device_id_type=MESH)

    others = [lax.rem(grp + d, groups) for d in range(1, groups)]

    for q in range(2):
        def part_step(d, c, q=q):
            h = lax.rem(grp + d, groups)
            part_of(h, q)
            part_copy(h, d, groups - d - 1, q).start()
            return c

        lax.fori_loop(1, groups, part_step, 0)
    for q in range(2):
        part_of(grp, q)

    ones = jnp.ones((8, span), jnp.bfloat16)
    scale = 1.0 / math.sqrt(width)
    for c in range(groups):
        cols = slice(c * group_ex, (c + 1) * group_ex)
        acc = jnp.zeros((8, group_ex), jnp.float32)
        for r in range(ranks):
            right = recv[c * blocks:(c + 1) * blocks, pl.ds(r * examples, examples), :]
            acc += lax.dot_general(
                ones, right.reshape(group_ex, span), NT, preferred_element_type=jnp.float32)
        prow_part[:, cols] = acc * scale
    for h in others:
        prow_copy(h, grp).start()

    for q in range(2):
        for d, h in enumerate(others):
            part_copy(h, d + 1, d, q).wait_recv()
        mine = part[grp, cuts[q], :]
        for d in range(groups - 1):
            mine += landed[d, cuts[q], :]
        packs[grp, cuts[q], :] = mine
        for h in others:
            full_copy(h, grp, q).start()

    def arrive_stat(d, c):
        peer, pg, pb = peer_of(d)
        stat_copy(peer, pg, pb, peer).wait_recv()
        return c

    over_peers(arrive_stat)
    total = jnp.sum(jnp.sum(stats[...], axis=0)[:1, :], axis=1, keepdims=True)
    damping = damping_rate * total / (width * blocks)
    for h in others:
        prow_copy(h, h).wait_recv()
    first = prow_part[...]
    for h in others:
        first += prow_land[h]
    row[...] = first
    for h in others:
        for q in range(2):
            full_copy(h, h, q).wait_recv()
    for o in range(groups):
        here = slice(o * group_ex, (o + 1) * group_ex)
        for d in range(whole_blocks):
            there = (o + d) % groups
            there = slice(there * group_ex, (there + 1) * group_ex)
            entry = packs[o, d * group_ex:(d + 1) * group_ex, :]
            full[here, there] = entry
            if d:
                full[there, here] = entry.T
        if split:
            low = o % pair
            start = low * group_ex + o // pair * half_ex
            there = slice((low + pair) * group_ex, (low + pair + 1) * group_ex)
            entry = packs[o, whole_blocks * group_ex:, :]
            full[start:start + half_ex, there] = entry
            full[there, start:start + half_ex] = entry.T

    tile = 128
    tiles = total_ex // tile

    def tile_rows(i):
        return pl.ds(pl.multiple_of(i * tile, tile), tile)

    def turn(i, c):
        spot = lax.broadcasted_iota(jnp.int32, (tile, total_ex), 0) + i * tile
        lane = lax.broadcasted_iota(jnp.int32, (tile, total_ex), 1)
        picked = jnp.where(spot == lane, row[:1, :], 0.0)
        col[tile_rows(i), :] = jnp.broadcast_to(
            jnp.sum(picked, axis=1, keepdims=True), (tile, 128))
        return c

    lax.fori_loop(0, tiles, turn, 0)
    top = None
    for step in range(power_steps):
        last = step + 1 == power_steps
        prow = row[:1, :]

        def image(i, acc):
            k_tile = full[tile_rows(i), :]
            if not last:
                col_next[tile_rows(i), :] = jnp.broadcast_to(
                    jnp.sum(k_tile * prow, axis=1, keepdims=True), (tile, 128))
            return acc + jnp.sum(k_tile * col[tile_rows(i), :][:, :1], axis=0, keepdims=True)

        q = lax.fori_loop(0, tiles, image, jnp.zeros((1, total_ex), jnp.float32))
        square = jnp.sum(prow * q, axis=1, keepdims=True)
        top = jnp.sqrt(jnp.maximum(square, 0.0) + 1e-06)
        if not last:
            row[...] = jnp.broadcast_to(q / top, row.shape)
            col[...] = col_next[...] / top

    center = damping + top
    rho, delta = top / center, damping / center
    zero, one = jnp.zeros_like(center), jnp.ones_like(center)

    def shifted(p):
        low = [delta * v for v in p] + [zero]
        return [a + b for a, b in zip(low, [zero] + list(p))]

    def plus(p, q, factor):
        n = max(len(p), len(q))
        p = list(p) + [zero] * (n - len(p))
        q = list(q) + [zero] * (n - len(q))
        return [a + factor * b for a, b in zip(p, q)]

    sig = one
    direction = [one]
    solution_poly = [one]
    residual = plus([one], shifted(direction), -sig)
    for sweep in range(1, ITERS):
        momentum = 0.5 * (rho * sig) ** 2 if sweep == 1 else (0.5 * rho * sig) ** 2
        sig = 1.0 / (1.0 - momentum / sig)
        direction = plus(residual, direction, momentum)
        solution_poly = plus(solution_poly, direction, sig)
        if sweep + 1 < ITERS:
            residual = plus(residual, shifted(direction), -sig)
    s0, s1, s2, s3 = solution_poly

    inverse = 1.0 / center
    y_ref[...] = full[grp_rows(grp), :] * inverse
    own_cols = pl.ds(pl.multiple_of(grp * group_ex, group_ex), group_ex)
    sc[...] = s0 * y_ref[:, own_cols]
    step_ex = min(256, total_ex)

    def halves(v):
        high = v.astype(jnp.bfloat16)
        return high, (v - high.astype(jnp.float32)).astype(jnp.bfloat16)

    def dot_nt(a, b):
        def product(x, y):
            return lax.dot_general(x, y, NT, preferred_element_type=jnp.float32)

        (a_high, a_low), (b_high, b_low) = halves(a), halves(b)
        return product(a_high, b_high) + (product(a_high, b_low) + product(a_low, b_high))

    def solve(j, c):
        at = pl.ds(pl.multiple_of(j * step_ex, step_ex), step_ex)
        y_tile = y_ref[:, at]
        z_tile = dot_nt(y_ref[...], full[at, :] * inverse)
        sc[...] += dot_nt(y_tile, s1 * y_tile + s2 * z_tile) + dot_nt(z_tile, s3 * z_tile)
        return c

    lax.fori_loop(0, total_ex // step_ex, solve, 0)

    def score_copy(b, slot):
        start = pl.multiple_of(b * examples, examples)
        return pltpu.make_async_remote_copy(
            src_ref=sc.at[pl.ds(start, examples)], dst_ref=sc_land.at[slot],
            send_sem=s_send.at[b], recv_sem=s_recv.at[slot],
            device_id=(grp, b), device_id_type=MESH)

    def score_send(d, c):
        b = lax.rem(blk + d, blocks)
        score_copy(b, blk).start()
        return c

    lax.fori_loop(1, blocks, score_send, 0)
    sc_land[blk] = sc[pl.ds(pl.multiple_of(blk * examples, examples), examples), :]

    def score_arrive(d, c):
        b = lax.rem(blk + d, blocks)
        score_copy(b, b).wait_recv()
        return c

    lax.fori_loop(1, blocks, score_arrive, 0)
    out_ref[...] = jnp.sum(sc_land[...], axis=0)

    def sent(d, c):
        peer, pg, pb = peer_of(d)
        feature_copy(peer, pg, pb, me).wait_send()
        stat_copy(peer, pg, pb, me).wait_send()
        return c

    over_peers(sent)
    for d, h in enumerate(others):
        for q in range(2):
            part_copy(h, d + 1, groups - d - 2, q).wait_send()
            full_copy(h, grp, q).wait_send()
    for h in others:
        prow_copy(h, grp).wait_send()

    def score_sent(d, c):
        score_copy(lax.rem(blk + d, blocks), blk).wait_send()
        return c

    lax.fori_loop(1, blocks, score_sent, 0)


def shards(groups, blocks, activations, out_grads, proj_act, proj_out):
    examples = activations.shape[0] // SEQ
    rank, span = proj_act.shape[1], proj_out.shape[1]
    devices = groups * blocks
    group_ex, total_ex = examples * blocks, examples * devices
    ranks = rank // devices
    width = rank * span // blocks
    act_low = jnp.dot(activations, proj_act, preferred_element_type=jnp.float32).astype(
        jnp.bfloat16
    )
    grad_low = jnp.dot(out_grads, proj_out, preferred_element_type=jnp.float32).astype(jnp.bfloat16)
    vmem = pl.BlockSpec(memory_space=pltpu.VMEM)
    f32 = jnp.float32
    dma = pltpu.SemaphoreType.DMA
    keep = group_ex * ((groups - 1) // 2 + 1) + (0 if groups % 2 else group_ex // 2)
    scores = pl.pallas_call(
        functools.partial(mix_kernel, groups, blocks, examples, ranks, width),
        out_shape=jax.ShapeDtypeStruct((examples, group_ex), f32),
        in_specs=[vmem] * 2,
        out_specs=vmem,
        scratch_shapes=[
            pltpu.VMEM((span // 128, rank * examples, 128), f32),
            pltpu.VMEM((devices, ranks * examples, span), jnp.bfloat16),
            pltpu.VMEM((8, 128), f32),
            pltpu.VMEM((devices, ranks * examples, span), jnp.bfloat16),
            pltpu.VMEM((devices, 8, 128), f32),
            pltpu.VMEM((groups, keep, group_ex), f32),
            pltpu.VMEM((groups - 1, keep, group_ex), f32),
            pltpu.VMEM((groups, keep, group_ex), f32),
            pltpu.VMEM((total_ex, total_ex), f32),
            pltpu.VMEM((8, total_ex), f32),
            pltpu.VMEM((groups, 8, total_ex), f32),
            pltpu.VMEM((8, total_ex), f32),
            pltpu.VMEM((total_ex, 128), f32),
            pltpu.VMEM((total_ex, 128), f32),
            pltpu.VMEM((group_ex, total_ex), f32),
            pltpu.VMEM((group_ex, group_ex), f32),
            pltpu.VMEM((blocks, examples, group_ex), f32),
            dma((devices,)), dma((devices,)), dma((devices,)), dma((devices,)),
            dma((2 * groups,)), dma((2 * groups,)), dma((2 * groups,)), dma((2 * groups,)),
            dma((groups,)), dma((groups,)), dma((blocks,)), dma((blocks,)),
        ],
        compiler_params=pltpu.CompilerParams(
            collective_id=0, has_side_effects=True, vmem_limit_bytes=67043328
        ),
    )(act_low, grad_low)
    return scores * float(examples * groups)


def solution(mesh):
    in_specs = (P(("grp", "blk"), None), P(("grp", "blk"), None), P(), P())
    out_specs = P(("grp", "blk"), None)
    body = functools.partial(shards, mesh.shape["grp"], mesh.shape["blk"])
    return jax.shard_map(body, mesh=mesh, in_specs=in_specs, out_specs=out_specs, check_vma=False)
```

```python
import functools
import math

import jax
import jax.numpy as jnp
from jax import lax
from jax.experimental import pallas as pl
from jax.experimental.pallas import tpu as pltpu
from jax.sharding import PartitionSpec as P

SEQ = 64
ITERS = 4
damping_rate = 0.5
power_steps = 3
MESH = pl.DeviceIdType.MESH
NT = (((1,), (1,)), ((), ()))
TN = (((0,), (0,)), ((), ()))


def mix_kernel(
    groups, blocks, examples, ranks, width,
    act_ref, grad_ref, out_ref,
    wide, feat_ref, stat_ref, recv, stats, part, landed, packs, full, prow_part, prow_land, row, col, col_next,
    y_ref, sc, sc_land,
    f_send, f_recv, t_send, t_recv, r_send, r_recv, g_send, g_recv, p_send, p_recv, s_send, s_recv,
):
    devices = groups * blocks
    group_ex = examples * blocks
    total_ex = group_ex * groups
    span = recv.shape[2]
    rows_out = ranks * examples
    grp, blk = lax.axis_index("grp"), lax.axis_index("blk")
    me = grp * blocks + blk

    half = blocks // 2 * groups

    def peer_of(d):
        pg = lax.rem(grp + lax.rem(d, groups), groups)
        pb = lax.rem(blk + blocks // 2 + d // groups, blocks)
        return pg * blocks + pb, pg, pb

    def over_peers(step):
        lax.fori_loop(0, half, step, 0)
        lax.fori_loop(half + 1, devices, step, 0)

    barrier = pltpu.get_barrier_semaphore()

    def greet(d, c):
        _, pg, pb = peer_of(d)
        pl.semaphore_signal(barrier, inc=1, device_id=(pg, pb), device_id_type=MESH)
        return c

    over_peers(greet)
    for e in range(examples):
        tokens = pl.ds(e * SEQ, SEQ)
        product = lax.dot_general(
            act_ref[tokens, :], grad_ref[tokens, :], TN, preferred_element_type=jnp.float32
        )
        for c in range(wide.shape[0]):
            wide[c, pl.ds(e, act_ref.shape[1], stride=examples), :] = (
                product[:, c * 128:(c + 1) * 128])
    stat_ref[...] = jnp.zeros_like(stat_ref)
    pl.semaphore_wait(barrier, devices - 1)

    def feature_copy(dest, pg, pb, slot):
        return pltpu.make_async_remote_copy(
            src_ref=feat_ref.at[pb * groups + pg], dst_ref=recv.at[slot],
            send_sem=f_send.at[dest], recv_sem=f_recv.at[slot],
            device_id=(pg, pb), device_id_type=MESH)

    def stat_copy(dest, pg, pb, slot):
        return pltpu.make_async_remote_copy(
            src_ref=stat_ref, dst_ref=stats.at[slot],
            send_sem=t_send.at[dest], recv_sem=t_recv.at[slot],
            device_id=(pg, pb), device_id_type=MESH)

    def narrow(pg, pb):
        slot = pb * groups + pg
        rows = pl.ds(pl.multiple_of(slot * rows_out, rows_out), rows_out)
        for c in range(wide.shape[0]):
            low = wide[c, rows, :].astype(jnp.bfloat16)
            feat_ref[slot, :, c * 128:(c + 1) * 128] = low
            back = low.astype(jnp.float32)
            square = jnp.sum(back * back, axis=0, keepdims=True)
            stat_ref[...] += jnp.broadcast_to(square, stat_ref.shape)

    def send(d, c):
        peer, pg, pb = peer_of(d)
        narrow(pg, pb)
        feature_copy(peer, pg, pb, me).start()
        return c

    over_peers(send)
    narrow(grp, blk)
    recv[me] = feat_ref[blk * groups + grp]

    def send_stat(d, c):
        peer, pg, pb = peer_of(d)
        stat_copy(peer, pg, pb, me).start()
        return c

    over_peers(send_stat)
    stats[me] = stat_ref[...]

    def arrive(d, c):
        peer, pg, pb = peer_of(d)
        feature_copy(peer, pg, pb, peer).wait_recv()
        return c

    over_peers(arrive)

    def grp_rows(h):
        return pl.ds(pl.multiple_of(h * group_ex, group_ex), group_ex)

    split = groups % 2 == 0
    whole_blocks = (groups - 1) // 2 + 1
    pair = groups // 2
    half_ex = group_ex // 2

    def block_into(h, at, left_at, left_n, right_at):
        for r in range(ranks):
            here = pl.ds(r * examples, examples)
            left = recv[pl.ds(left_at, left_n), here, :].reshape(left_n * examples, span)
            right = recv[pl.ds(right_at, blocks), here, :].reshape(group_ex, span)
            term = lax.dot_general(left, right, NT, preferred_element_type=jnp.float32)
            if r == 0:
                part[h, at:at + left_n * examples, :] = term
            else:
                part[h, at:at + left_n * examples, :] += term

    def part_of(h, q):
        if q < whole_blocks:
            block_into(h, q * group_ex, h * blocks, blocks, lax.rem(h + q, groups) * blocks)
        else:
            low = lax.rem(h, pair)
            block_into(h, whole_blocks * group_ex,
                       low * blocks + h // pair * (blocks // 2), blocks // 2,
                       (low + pair) * blocks)

    chunks = whole_blocks + int(split)
    cuts = [slice(q * group_ex, min((q + 1) * group_ex, part.shape[1])) for q in range(chunks)]

    def part_copy(h, d, slot, q):
        return pltpu.make_async_remote_copy(
            src_ref=part.at[h, cuts[q]], dst_ref=landed.at[slot, cuts[q]],
            send_sem=r_send.at[chunks * d + q], recv_sem=r_recv.at[chunks * slot + q],
            device_id=(h, blk), device_id_type=MESH)

    def full_copy(h, slot, q):
        return pltpu.make_async_remote_copy(
            src_ref=packs.at[slot, cuts[q]], dst_ref=packs.at[slot, cuts[q]],
            send_sem=g_send.at[chunks * h + q], recv_sem=g_recv.at[chunks * slot + q],
            device_id=(h, blk), device_id_type=MESH)

    def prow_copy(h, slot):
        return pltpu.make_async_remote_copy(
            src_ref=prow_part, dst_ref=prow_land.at[slot],
            send_sem=p_send.at[h], recv_sem=p_recv.at[slot],
            device_id=(h, blk), device_id_type=MESH)

    others = [lax.rem(grp + d, groups) for d in range(1, groups)]

    for q in range(chunks):
        def part_step(d, c, q=q):
            h = lax.rem(grp + d, groups)
            part_of(h, q)
            part_copy(h, d, groups - d - 1, q).start()
            return c

        lax.fori_loop(1, groups, part_step, 0)
    for q in range(chunks):
        part_of(grp, q)

    ones = jnp.ones((8, span), jnp.bfloat16)
    scale = 1.0 / math.sqrt(width)
    for c in range(groups):
        cols = slice(c * group_ex, (c + 1) * group_ex)
        acc = jnp.zeros((8, group_ex), jnp.float32)
        for r in range(ranks):
            right = recv[c * blocks:(c + 1) * blocks, pl.ds(r * examples, examples), :]
            acc += lax.dot_general(
                ones, right.reshape(group_ex, span), NT, preferred_element_type=jnp.float32)
        prow_part[:, cols] = acc * scale
    for h in others:
        prow_copy(h, grp).start()

    for q in range(chunks):
        for d, h in enumerate(others):
            part_copy(h, d + 1, d, q).wait_recv()
        mine = part[grp, cuts[q], :]
        for d in range(groups - 1):
            mine += landed[d, cuts[q], :]
        packs[grp, cuts[q], :] = mine
        for h in others:
            full_copy(h, grp, q).start()

    def arrive_stat(d, c):
        peer, pg, pb = peer_of(d)
        stat_copy(peer, pg, pb, peer).wait_recv()
        return c

    over_peers(arrive_stat)
    total = jnp.sum(jnp.sum(stats[...], axis=0)[:1, :], axis=1, keepdims=True)
    damping = damping_rate * total / (width * blocks)
    for h in others:
        prow_copy(h, h).wait_recv()
    first = prow_part[...]
    for h in others:
        first += prow_land[h]
    row[...] = first
    for h in others:
        for q in range(chunks):
            full_copy(h, h, q).wait_recv()
    for o in range(groups):
        here = slice(o * group_ex, (o + 1) * group_ex)
        for d in range(whole_blocks):
            there = (o + d) % groups
            there = slice(there * group_ex, (there + 1) * group_ex)
            entry = packs[o, d * group_ex:(d + 1) * group_ex, :]
            full[here, there] = entry
            if d:
                full[there, here] = entry.T
        if split:
            low = o % pair
            start = low * group_ex + o // pair * half_ex
            there = slice((low + pair) * group_ex, (low + pair + 1) * group_ex)
            entry = packs[o, whole_blocks * group_ex:, :]
            full[start:start + half_ex, there] = entry
            full[there, start:start + half_ex] = entry.T

    tile = 128
    tiles = total_ex // tile

    def tile_rows(i):
        return pl.ds(pl.multiple_of(i * tile, tile), tile)

    def turn(i, c):
        spot = lax.broadcasted_iota(jnp.int32, (tile, total_ex), 0) + i * tile
        lane = lax.broadcasted_iota(jnp.int32, (tile, total_ex), 1)
        picked = jnp.where(spot == lane, row[:1, :], 0.0)
        col[tile_rows(i), :] = jnp.broadcast_to(
            jnp.sum(picked, axis=1, keepdims=True), (tile, 128))
        return c

    lax.fori_loop(0, tiles, turn, 0)
    top = None
    for step in range(power_steps):
        last = step + 1 == power_steps
        prow = row[:1, :]

        def image(i, acc):
            k_tile = full[tile_rows(i), :]
            if not last:
                col_next[tile_rows(i), :] = jnp.broadcast_to(
                    jnp.sum(k_tile * prow, axis=1, keepdims=True), (tile, 128))
            return acc + jnp.sum(k_tile * col[tile_rows(i), :][:, :1], axis=0, keepdims=True)

        q = lax.fori_loop(0, tiles, image, jnp.zeros((1, total_ex), jnp.float32))
        square = jnp.sum(prow * q, axis=1, keepdims=True)
        top = jnp.sqrt(jnp.maximum(square, 0.0) + 1e-06)
        if not last:
            row[...] = jnp.broadcast_to(q / top, row.shape)
            col[...] = col_next[...] / top

    center = damping + top
    rho, delta = top / center, damping / center
    zero, one = jnp.zeros_like(center), jnp.ones_like(center)

    def shifted(p):
        low = [delta * v for v in p] + [zero]
        return [a + b for a, b in zip(low, [zero] + list(p))]

    def plus(p, q, factor):
        n = max(len(p), len(q))
        p = list(p) + [zero] * (n - len(p))
        q = list(q) + [zero] * (n - len(q))
        return [a + factor * b for a, b in zip(p, q)]

    sig = one
    direction = [one]
    solution_poly = [one]
    residual = plus([one], shifted(direction), -sig)
    for sweep in range(1, ITERS):
        momentum = 0.5 * (rho * sig) ** 2 if sweep == 1 else (0.5 * rho * sig) ** 2
        sig = 1.0 / (1.0 - momentum / sig)
        direction = plus(residual, direction, momentum)
        solution_poly = plus(solution_poly, direction, sig)
        if sweep + 1 < ITERS:
            residual = plus(residual, shifted(direction), -sig)
    s0, s1, s2, s3 = solution_poly

    inverse = 1.0 / center
    y_ref[...] = full[grp_rows(grp), :] * inverse
    own_cols = pl.ds(pl.multiple_of(grp * group_ex, group_ex), group_ex)
    sc[...] = s0 * y_ref[:, own_cols]
    step_ex = min(256, total_ex)

    def halves(v):
        high = v.astype(jnp.bfloat16)
        return high, (v - high.astype(jnp.float32)).astype(jnp.bfloat16)

    def dot_nt(a, b):
        def product(x, y):
            return lax.dot_general(x, y, NT, preferred_element_type=jnp.float32)

        (a_high, a_low), (b_high, b_low) = halves(a), halves(b)
        return product(a_high, b_high) + (product(a_high, b_low) + product(a_low, b_high))

    def solve(j, c):
        at = pl.ds(pl.multiple_of(j * step_ex, step_ex), step_ex)
        y_tile = y_ref[:, at]
        z_tile = dot_nt(y_ref[...], full[at, :] * inverse)
        sc[...] += dot_nt(y_tile, s1 * y_tile + s2 * z_tile) + dot_nt(z_tile, s3 * z_tile)
        return c

    lax.fori_loop(0, total_ex // step_ex, solve, 0)

    def score_copy(b, slot):
        start = pl.multiple_of(b * examples, examples)
        return pltpu.make_async_remote_copy(
            src_ref=sc.at[pl.ds(start, examples)], dst_ref=sc_land.at[slot],
            send_sem=s_send.at[b], recv_sem=s_recv.at[slot],
            device_id=(grp, b), device_id_type=MESH)

    def score_send(d, c):
        b = lax.rem(blk + d, blocks)
        score_copy(b, blk).start()
        return c

    lax.fori_loop(1, blocks, score_send, 0)
    sc_land[blk] = sc[pl.ds(pl.multiple_of(blk * examples, examples), examples), :]

    def score_arrive(d, c):
        b = lax.rem(blk + d, blocks)
        score_copy(b, b).wait_recv()
        return c

    lax.fori_loop(1, blocks, score_arrive, 0)
    out_ref[...] = jnp.sum(sc_land[...], axis=0)

    def sent(d, c):
        peer, pg, pb = peer_of(d)
        feature_copy(peer, pg, pb, me).wait_send()
        stat_copy(peer, pg, pb, me).wait_send()
        return c

    over_peers(sent)
    for d, h in enumerate(others):
        for q in range(chunks):
            part_copy(h, d + 1, groups - d - 2, q).wait_send()
            full_copy(h, grp, q).wait_send()
    for h in others:
        prow_copy(h, grp).wait_send()

    def score_sent(d, c):
        score_copy(lax.rem(blk + d, blocks), blk).wait_send()
        return c

    lax.fori_loop(1, blocks, score_sent, 0)


def shards(groups, blocks, activations, out_grads, proj_act, proj_out):
    examples = activations.shape[0] // SEQ
    rank, span = proj_act.shape[1], proj_out.shape[1]
    devices = groups * blocks
    group_ex, total_ex = examples * blocks, examples * devices
    ranks = rank // devices
    width = rank * span // blocks
    act_low = jnp.dot(activations, proj_act, preferred_element_type=jnp.float32).astype(
        jnp.bfloat16
    )
    grad_low = jnp.dot(out_grads, proj_out, preferred_element_type=jnp.float32).astype(jnp.bfloat16)
    vmem = pl.BlockSpec(memory_space=pltpu.VMEM)
    f32 = jnp.float32
    dma = pltpu.SemaphoreType.DMA
    keep = group_ex * ((groups - 1) // 2 + 1) + (0 if groups % 2 else group_ex // 2)
    scores = pl.pallas_call(
        functools.partial(mix_kernel, groups, blocks, examples, ranks, width),
        out_shape=jax.ShapeDtypeStruct((examples, group_ex), f32),
        in_specs=[vmem] * 2,
        out_specs=vmem,
        scratch_shapes=[
            pltpu.VMEM((span // 128, rank * examples, 128), f32),
            pltpu.VMEM((devices, ranks * examples, span), jnp.bfloat16),
            pltpu.VMEM((8, 128), f32),
            pltpu.VMEM((devices, ranks * examples, span), jnp.bfloat16),
            pltpu.VMEM((devices, 8, 128), f32),
            pltpu.VMEM((groups, keep, group_ex), f32),
            pltpu.VMEM((groups - 1, keep, group_ex), f32),
            pltpu.VMEM((groups, keep, group_ex), f32),
            pltpu.VMEM((total_ex, total_ex), f32),
            pltpu.VMEM((8, total_ex), f32),
            pltpu.VMEM((groups, 8, total_ex), f32),
            pltpu.VMEM((8, total_ex), f32),
            pltpu.VMEM((total_ex, 128), f32),
            pltpu.VMEM((total_ex, 128), f32),
            pltpu.VMEM((group_ex, total_ex), f32),
            pltpu.VMEM((group_ex, group_ex), f32),
            pltpu.VMEM((blocks, examples, group_ex), f32),
            dma((devices,)), dma((devices,)), dma((devices,)), dma((devices,)),
            dma((groups * groups,)), dma((groups * groups,)), dma((groups * groups,)), dma((groups * groups,)),
            dma((groups,)), dma((groups,)), dma((blocks,)), dma((blocks,)),
        ],
        compiler_params=pltpu.CompilerParams(
            collective_id=0, has_side_effects=True, vmem_limit_bytes=67043328
        ),
    )(act_low, grad_low)
    return scores * float(examples * groups)


def solution(mesh):
    in_specs = (P(("grp", "blk"), None), P(("grp", "blk"), None), P(), P())
    out_specs = P(("grp", "blk"), None)
    body = functools.partial(shards, mesh.shape["grp"], mesh.shape["blk"])
    return jax.shard_map(body, mesh=mesh, in_specs=in_specs, out_specs=out_specs, check_vma=False)
```
